512 devices in a mesh: row: 16 (over y, x_lo), col: 16 (over z, x_hi), depth: 2 (over core).
Axes of the slice: x: 4 (x_hi: 2, x_lo: 2; x = x_hi * 2 + x_lo), y: 8, z: 8, core: 2. Of those that a mesh axis runs over, the one named last changes fastest.
Arguments:
- grad_out: bfloat16 [4096, 8192], P('col', 'row'), may hold values from -6 to 6
- hidden: bfloat16 [4096, 14336], P('row', 'col'), may hold values from -0.25 to 0.25
- weight: bfloat16 [8192, 14336], P('row', 'col'), may hold values from -0.046875 to 0.046875
Outputs:
- grad_hidden: bfloat16 [4096, 14336], P('row', 'col')
- grad_weight: bfloat16 [8192, 14336], P('row', 'col')
The draws below stay inside these ranges and needn't reach their ends.
All inputs are finite; a program needn't handle non-finite values.
Results may differ from the reference program's by a relative error of at most 0.0034.
Values may be sent and summed in bfloat16 or wider, within the bound.
A program may use at most 64 MiB of HBM per device.

```python
import jax
import jax.numpy as jnp
from jax import lax

D = 8192
FFW = 14336
TOKENS = 4096


def levels(key, shape, shards, smallest, largest):
    level, own = 1.0, jax.random.fold_in(key, 6)
    for dim, shards_of in shards:
        draws = jnp.exp(jax.random.uniform(jax.random.fold_in(own, dim), (shards_of,), jnp.float32, smallest / len(shards), largest / len(shards)))
        level = level * jnp.repeat(draws, shape[dim] // shards_of).reshape([-1 if axis == dim else 1 for axis in range(len(shape))])
    return level


def noise(own_key, extent, spread, most, split=(), held_as=jnp.bfloat16):
    drawn = jax.random.normal(own_key, extent, jnp.float32) * spread
    if len(split) > 0:
        drawn = levels(own_key, extent, split, -0.22, 0.18) * drawn
    return jnp.clip(drawn, min=-most, max=most).astype(held_as)


def setup_inputs(seed: int = 0) -> dict:
    seeds = jax.random.split(jax.random.key(seed), 4)
    return {
        "grad_out": noise(seeds[0], (TOKENS, D), 1.0, 6.0, ((0, 16), (1, 16))),
        "hidden": noise(seeds[1], (TOKENS, FFW), (TOKENS ** -0.5), 0.25, ((0, 16), (1, 16))),
        "weight": noise(seeds[2], (D, FFW), FFW ** -0.5, 0.046875, ((0, 16), (1, 16))),
    }


def reference(grad_out, hidden, weight):
    grad_hidden = jnp.dot(grad_out, weight, preferred_element_type=jnp.float32).astype(jnp.bfloat16)
    grad_weight = lax.dot_general(grad_out, hidden, (((0,), (0,)), ((), ())), preferred_element_type=jnp.float32).astype(jnp.bfloat16)
    return grad_hidden, grad_weight
```

```python
import jax
import jax.numpy as jnp
from jax import lax
from jax.experimental import pallas as pl
from jax.experimental.pallas import tpu as pltpu
from jax.sharding import PartitionSpec as P

MESH = pl.DeviceIdType.MESH
BF16, F32 = jnp.bfloat16, jnp.float32
RING = 8
HOPS = [
    (sign, other, hop)
    for hop in (1, 2, 3, 4)
    for other in (0, 1)
    for sign in (1, -1)
    if hop < 4 or (sign == 1) == (other == 0)
]


def wrap(pos):
    return lax.rem(pos + RING, RING)


class Gather:
    def __init__(self, axis, own, full, send, recv):
        at = lax.axis_index(axis)
        self.axis, self.own, self.full, self.send, self.recv = axis, own, full, send, recv
        self.pos, self.lane = at // 2, lax.rem(at, 2)

    def device(self, pos, lane):
        return {self.axis: wrap(pos) * 2 + lane}

    def slot(self, pos, lane):
        return wrap(pos) * 2 + lane

    def copy(self, src, slot, key, device):
        return pltpu.make_async_remote_copy(
            src_ref=src,
            dst_ref=self.full.at[slot],
            send_sem=self.send.at[key],
            recv_sem=self.recv.at[key],
            device_id=device,
            device_id_type=MESH,
        )

    def swap(self):
        slot = self.slot(self.pos, self.lane)
        return self.copy(self.own, slot, len(HOPS), self.device(self.pos, 1 - self.lane))

    def swapped(self):
        slot = self.slot(self.pos, 1 - self.lane)
        device = self.device(self.pos, 1 - self.lane)
        self.copy(self.full.at[slot], slot, len(HOPS), device).wait_recv()

    def hop(self, sign, other, hop):
        lane = 1 - self.lane if other else self.lane
        slot = self.slot(self.pos - sign * (hop - 1), lane)
        src = self.own if hop == 1 and not other else self.full.at[slot]
        key = HOPS.index((sign, other, hop))
        return self.copy(src, slot, key, self.device(self.pos + sign, self.lane))

    def arrived(self, sign, other, hop):
        lane = 1 - self.lane if other else self.lane
        slot = self.slot(self.pos - sign * hop, lane)
        key = HOPS.index((sign, other, hop))
        device = self.device(self.pos - sign, self.lane)
        self.copy(self.full.at[slot], slot, key, device).wait_recv()

    def round(self, hop, sent):
        for sign, other, step in HOPS:
            if step == hop:
                self.arrived(sign, other, hop)
                if (sign, other, hop + 1) in HOPS:
                    sent.append(self.hop(sign, other, hop + 1))
                    sent[-1].start()


def kernel(
    g_ref, h_ref, w_ref, gh_ref, gw_ref,
    ga, ha, kept, xs, xr, ys, yr, acc, acc_in, half_s, half_r,
    g_send, g_recv, h_send, h_recv, x_send, x_recv, y_send, y_recv, d_send, d_recv,
):
    depth = lax.axis_index("depth")
    half = g_ref.shape[0] // 2
    quarter = half // 2
    mine = pl.ds(pl.multiple_of(depth * half, half), half)
    gathers = (
        Gather("col", g_ref.at[mine], ga, g_send, g_recv),
        Gather("row", h_ref.at[mine], ha, h_send, h_recv),
    )
    grad, hidden = gathers
    y, lane = hidden.pos, hidden.lane

    def row_device(pos):
        return {"row": wrap(pos) * 2 + lane}

    partner = {"row": y * 2 + 1 - lane}
    sibling = {"depth": 1 - depth}

    barrier = pltpu.get_barrier_semaphore()
    peers = [partner, sibling, grad.device(grad.pos, 1 - grad.lane)]
    peers += [grad.device(grad.pos + k, grad.lane) for k in (-1, 1)]
    peers += [row_device(y + k) for k in (-3, -2, -1, 1, 2, 3)]
    for peer in peers:
        pl.semaphore_signal(barrier, inc=1, device_id=peer, device_id_type=MESH)
    pl.semaphore_wait(barrier, len(peers))

    sent = []

    def start(copy):
        copy.start()
        sent.append(copy)

    for gather in gathers:
        start(gather.swap())
        for sign in (1, -1):
            start(gather.hop(sign, 0, 1))
    for gather in gathers:
        gather.full[gather.slot(gather.pos, gather.lane)] = gather.own[...]

    def across(pos, at):
        pos = wrap(pos)
        return pltpu.make_async_remote_copy(
            src_ref=xs.at[pos],
            dst_ref=xr.at[pos],
            send_sem=x_send.at[at],
            recv_sem=x_recv.at[at],
            device_id=partner,
            device_id_type=MESH,
        )

    def product(pos, at):
        pos = wrap(pos)
        away = jnp.dot(ga[pos * 2 + 1 - lane], w_ref[...], preferred_element_type=F32)
        xs[pos] = away.astype(BF16)
        start(across(pos, at))
        kept[pos] = jnp.dot(ga[pos * 2 + lane], w_ref[...], preferred_element_type=F32)

    def products(hop):
        product(grad.pos - hop, 2 * hop - 1)
        if hop < 4:
            product(grad.pos + hop, 2 * hop)

    def second_lane(gather):
        gather.swapped()
        for sign in (1, -1):
            start(gather.hop(sign, 1, 1))

    second_lane(grad)
    product(grad.pos, 0)
    second_lane(hidden)
    grad.round(1, sent)
    products(1)
    hidden.round(1, sent)
    grad.round(2, sent)
    products(2)
    grad.round(3, sent)
    products(3)
    hidden.round(2, sent)
    grad.round(4, sent)
    products(4)
    hidden.round(3, sent)

    for hop in range(5):
        across(grad.pos - hop, max(2 * hop - 1, 0)).wait_recv()
        if 0 < hop < 4:
            across(grad.pos + hop, 2 * hop).wait_recv()

    def total(pos, rows):
        pos = wrap(pos)
        return kept[pos, rows] + xr[pos, rows].astype(F32)

    plans, at = [], 0
    for sign in (1, -1):
        for part in (0, 1):
            far = 4 if (part == 0) == (sign == 1) else 3
            plans.append((sign, pl.ds(part * quarter, quarter), far, at, part))
            at += far

    def along(key, pos):
        return pltpu.make_async_remote_copy(
            src_ref=ys.at[key],
            dst_ref=yr.at[key],
            send_sem=y_send.at[key],
            recv_sem=y_recv.at[key],
            device_id=row_device(pos),
            device_id_type=MESH,
        )

    def emit(key, value, pos):
        ys[key] = value.astype(BF16)
        start(along(key, pos))

    for sign, rows, far, key, _ in plans:
        emit(key, total(y + sign * far, rows), y + sign)
    for sign, rows, far, key, _ in plans:
        if far == 4:
            emit(key + 2, total(y + sign * 2, rows), y + sign)
    for sign, rows, far, key, _ in plans:
        if far == 3:
            emit(key + 2, total(y + sign, rows), y + sign)

    hidden.round(4, sent)

    for sign, rows, far, key, _ in plans:
        along(key, y).wait_recv()
        value = total(y + sign * (far - 1), rows) + yr[key].astype(F32)
        emit(key + 1, value, y + sign * (far - 1))
    for sign, rows, far, key, _ in plans:
        if far == 4:
            along(key + 2, y).wait_recv()
            value = total(y + sign, rows) + yr[key + 2].astype(F32)
            emit(key + 3, value, y + sign)

    acc[...] = jnp.zeros_like(acc)
    chunk = 4

    @pl.loop(0, 2 * RING // chunk)
    def _(step):
        tokens = pl.ds(step * chunk, chunk)
        left = ga[tokens].reshape(chunk * half, -1)
        right = ha[tokens].reshape(chunk * half, -1)
        acc[...] += lax.dot_general(
            left, right, (((0,), (0,)), ((), ())), preferred_element_type=F32
        )

    def to_sibling(src, dst, key):
        return pltpu.make_async_remote_copy(
            src_ref=src,
            dst_ref=dst,
            send_sem=d_send.at[key],
            recv_sem=d_recv.at[key],
            device_id=sibling,
            device_id_type=MESH,
        )

    weight_swap = to_sibling(acc, acc_in, 0)
    start(weight_swap)
    weight_swap.wait_recv()
    gw_ref[...] = (acc[...] + acc_in[...]).astype(BF16)

    for part in (0, 1):
        rows = pl.ds(part * quarter, quarter)
        value = total(y, rows)
        for sign, _, far, key, which in plans:
            if which == part:
                for last in (key + 1, key + 3 if far == 4 else key + 2):
                    along(last, y).wait_recv()
                    value += yr[last].astype(F32)
        half_s[rows] = value.astype(BF16)
    half_swap = to_sibling(half_s, half_r, 1)
    start(half_swap)
    gh_ref[mine] = half_s[...]
    half_swap.wait_recv()
    gh_ref[pl.ds(pl.multiple_of((1 - depth) * half, half), half)] = half_r[...]
    for copy in sent:
        copy.wait_send()


def body(grad_out, hidden, weight):
    (tokens, features), units = grad_out.shape, hidden.shape[1]
    half, quarter, blocks = tokens // 2, tokens // 4, 2 * RING
    dma = pltpu.SemaphoreType.DMA
    vmem = pl.BlockSpec(memory_space=pltpu.VMEM)
    swaps = len(HOPS) + 1
    return pl.pallas_call(
        kernel,
        out_shape=(
            jax.ShapeDtypeStruct(hidden.shape, BF16),
            jax.ShapeDtypeStruct(weight.shape, BF16),
        ),
        in_specs=[vmem] * 3,
        out_specs=(vmem, vmem),
        scratch_shapes=[
            pltpu.VMEM((blocks, half, features), BF16),
            pltpu.VMEM((blocks, half, units), BF16),
            pltpu.VMEM((RING, half, units), F32),
            pltpu.VMEM((RING, half, units), BF16),
            pltpu.VMEM((RING, half, units), BF16),
            pltpu.VMEM((14, quarter, units), BF16),
            pltpu.VMEM((14, quarter, units), BF16),
            pltpu.VMEM((features, units), F32),
            pltpu.VMEM((features, units), F32),
            pltpu.VMEM((half, units), BF16),
            pltpu.VMEM((half, units), BF16),
            dma((swaps,)), dma((swaps,)), dma((swaps,)), dma((swaps,)),
            dma((RING,)), dma((RING,)), dma((14,)), dma((14,)), dma((2,)), dma((2,)),
        ],
        compiler_params=pltpu.CompilerParams(
            collective_id=0, has_side_effects=True, vmem_limit_bytes=56 << 20
        ),
    )(grad_out, hidden, weight)


def solution(mesh):
    return jax.shard_map(
        body,
        mesh=mesh,
        in_specs=(P("col", "row"), P("row", "col"), P("row", "col")),
        out_specs=(P("row", "col"), P("row", "col")),
        check_vma=False,
    )
```

```python
import jax
import jax.numpy as jnp
from jax import lax
from jax.experimental import pallas as pl
from jax.experimental.pallas import tpu as pltpu
from jax.sharding import PartitionSpec as P

MESH = pl.DeviceIdType.MESH
BF16, F32 = jnp.bfloat16, jnp.float32
RING = 8
GRAD_HOPS = [
    (sign, lane, hop)
    for hop in (1, 2, 3, 4)
    for lane in (0, 1, 2)
    for sign in (1, -1)
    if hop < 4 or (sign == 1) == (lane != 1)
]
HIDDEN_HOPS = [(1, 0, 1), (-1, 0, 1), (1, 0, 2), (-1, 0, 2), (1, 0, 3), (-1, 0, 3), (1, 0, 4)]
HIDDEN_HOPS += [(1, 1, 1), (-1, 1, 1), (-1, 1, 2)]
HANDED = [(1, 0, 2), (1, 0, 3), (-1, 0, 3), (1, 0, 4)]


def wrap(pos):
    return lax.rem(pos + RING, RING)


class Gather:
    def __init__(self, axis, hops, own, full, send, recv):
        at = lax.axis_index(axis)
        self.axis, self.hops, self.own, self.full = axis, hops, own, full
        self.send, self.recv = send, recv
        self.pos, self.lane = at // 2, lax.rem(at, 2)

    def device(self, pos, lane):
        return {self.axis: wrap(pos) * 2 + lane}

    def slot(self, pos, lane):
        if lane == 2:
            return 2 * RING + wrap(pos)
        return wrap(pos) * 2 + (1 - self.lane if lane else self.lane)

    def copy(self, src, slot, key, device):
        return pltpu.make_async_remote_copy(
            src_ref=src,
            dst_ref=self.full.at[slot],
            send_sem=self.send.at[key],
            recv_sem=self.recv.at[key],
            device_id=device,
            device_id_type=MESH,
        )

    def partner(self):
        return self.device(self.pos, 1 - self.lane)

    def swap(self):
        return self.copy(self.own, self.slot(self.pos, 0), len(self.hops), self.partner())

    def swapped(self):
        slot = self.slot(self.pos, 1)
        self.copy(self.full.at[slot], slot, len(self.hops), self.partner()).wait_recv()

    def hop(self, sign, lane, hop):
        slot = self.slot(self.pos - sign * (hop - 1), lane)
        src = self.own if hop == 1 and not lane else self.full.at[slot]
        key = self.hops.index((sign, lane, hop))
        return self.copy(src, slot, key, self.device(self.pos + sign, self.lane))

    def arrived(self, sign, lane, hop):
        slot = self.slot(self.pos - sign * hop, lane)
        key = self.hops.index((sign, lane, hop))
        device = self.device(self.pos - sign, self.lane)
        self.copy(self.full.at[slot], slot, key, device).wait_recv()

    def hand(self, index):
        sign, _, hop = HANDED[index]
        slot = self.slot(self.pos - sign * hop, 0)
        return self.copy(self.full.at[slot], slot, len(self.hops) + 1 + index, self.partner())

    def handed(self, index):
        sign, _, hop = HANDED[index]
        slot = self.slot(self.pos - sign * hop, 1)
        key = len(self.hops) + 1 + index
        self.copy(self.full.at[slot], slot, key, self.partner()).wait_recv()


def kernel(
    g_ref, h_ref, w_ref, gh_ref, gw_ref,
    ga, ha, wo, kept, ys, yr, acc, acc_in, half_s, half_r,
    g_send, g_recv, h_send, h_recv, w_send, w_recv, y_send, y_recv, d_send, d_recv,
):
    depth = lax.axis_index("depth")
    half = g_ref.shape[0] // 2
    quarter = half // 2
    mine = pl.ds(pl.multiple_of(depth * half, half), half)
    grad = Gather("col", GRAD_HOPS, g_ref.at[mine], ga, g_send, g_recv)
    hidden = Gather("row", HIDDEN_HOPS, h_ref.at[mine], ha, h_send, h_recv)
    y, lane = hidden.pos, hidden.lane

    def row_device(pos):
        return {"row": wrap(pos) * 2 + lane}

    partner = hidden.partner()
    sibling = {"depth": 1 - depth}
    across = partner | grad.partner()

    barrier = pltpu.get_barrier_semaphore()
    peers = [partner, sibling, across, grad.partner()]
    peers += [grad.device(grad.pos + k, grad.lane) for k in (-1, 1)]
    peers += [row_device(y + k) for k in (-3, -2, -1, 1, 2, 3)]
    for peer in peers:
        pl.semaphore_signal(barrier, inc=1, device_id=peer, device_id_type=MESH)
    pl.semaphore_wait(barrier, len(peers))

    sent = []

    def start(copy):
        copy.start()
        sent.append(copy)

    lane_2 = len(GRAD_HOPS) + 1
    third = [grad.copy(grad.own, grad.slot(grad.pos, 2), lane_2 + i, to) for i, to in enumerate((partner, across))]

    def third_arrived():
        slot = grad.slot(grad.pos, 2)
        for i, (source, here) in enumerate(((partner, lane == grad.lane), (across, lane != grad.lane))):
            @pl.when(here)
            def _():
                grad.copy(ga.at[slot], slot, lane_2 + i, source).wait_recv()

    features = w_ref.shape[0] // 2
    part = pl.ds(pl.multiple_of(depth * features, features), features)
    rest = pl.ds(pl.multiple_of((1 - depth) * features, features), features)

    def weights(src, rows, key, device):
        return pltpu.make_async_remote_copy(
            src_ref=src.at[rows],
            dst_ref=wo.at[rows],
            send_sem=w_send.at[key],
            recv_sem=w_recv.at[key],
            device_id=device,
            device_id_type=MESH,
        )

    for sign in (1, -1):
        start(grad.hop(sign, 0, 1))
    @pl.when(lane != grad.lane)
    def _():
        for copy in third:
            copy.start()
    start(grad.swap())
    for sign in (1, -1):
        start(hidden.hop(sign, 0, 1))
    start(weights(w_ref, part, 0, partner))
    start(hidden.swap())
    for gather in (grad, hidden):
        gather.full[gather.slot(gather.pos, 0)] = gather.own[...]

    def grad_round(hop):
        for key in GRAD_HOPS:
            if key[2] == hop:
                grad.arrived(*key)
                following = (*key[:2], hop + 1)
                if following in GRAD_HOPS:
                    start(grad.hop(*following))

    def hidden_round(lane, hop):
        for key in HIDDEN_HOPS:
            if key[1:] == (lane, hop):
                hidden.arrived(*key)
                following = (*key[:2], hop + 1)
                if following in HIDDEN_HOPS:
                    start(hidden.hop(*following))
                if key in HANDED:
                    start(hidden.hand(HANDED.index(key)))

    def product(pos):
        pos = wrap(pos)
        value = jnp.dot(ga[pos * 2 + lane], w_ref[...], preferred_element_type=F32)
        kept[pos] = value + jnp.dot(ga[2 * RING + pos], wo[...], preferred_element_type=F32)

    def products(hop):
        product(grad.pos - hop)
        if hop < 4:
            product(grad.pos + hop)

    third_arrived()
    for sign in (1, -1):
        start(grad.hop(sign, 2, 1))
    grad.swapped()
    for sign in (1, -1):
        start(grad.hop(sign, 1, 1))
    hidden_round(0, 1)
    grad_round(1)
    weights(w_ref, part, 0, partner).wait_recv()
    start(weights(wo, part, 1, sibling))
    hidden_round(0, 2)
    hidden.swapped()
    for sign in (1, -1):
        start(hidden.hop(sign, 1, 1))
    weights(wo, rest, 1, sibling).wait_recv()
    product(grad.pos)
    products(1)
    grad_round(2)
    hidden_round(0, 3)
    products(2)
    hidden_round(1, 1)
    grad_round(3)
    products(3)
    hidden_round(0, 4)
    grad_round(4)
    products(4)

    def total(pos, rows):
        return kept[wrap(pos), rows]

    plans, at = [], 0
    for sign in (1, -1):
        for part in (0, 1):
            far = 4 if (part == 0) == (sign == 1) else 3
            plans.append((sign, pl.ds(part * quarter, quarter), far, at, part))
            at += far

    def along(key, pos):
        return pltpu.make_async_remote_copy(
            src_ref=ys.at[key],
            dst_ref=yr.at[key],
            send_sem=y_send.at[key],
            recv_sem=y_recv.at[key],
            device_id=row_device(pos),
            device_id_type=MESH,
        )

    def emit(key, value, pos):
        ys[key] = value.astype(BF16)
        start(along(key, pos))

    for sign, rows, far, key, _ in plans:
        emit(key, total(y + sign * far, rows), y + sign)
    for sign, rows, far, key, _ in plans:
        if far == 4:
            emit(key + 2, total(y + sign * 2, rows), y + sign)
    for sign, rows, far, key, _ in plans:
        if far == 3:
            emit(key + 2, total(y + sign, rows), y + sign)

    for sign, rows, far, key, _ in plans:
        along(key, y).wait_recv()
        value = total(y + sign * (far - 1), rows) + yr[key].astype(F32)
        emit(key + 1, value, y + sign * (far - 1))
    for sign, rows, far, key, _ in plans:
        if far == 4:
            along(key + 2, y).wait_recv()
            value = total(y + sign, rows) + yr[key + 2].astype(F32)
            emit(key + 3, value, y + sign)

    hidden_round(1, 2)
    for index in range(len(HANDED)):
        hidden.handed(index)
    acc[...] = jnp.zeros_like(acc)
    chunk = 4

    @pl.loop(0, 2 * RING // chunk)
    def _(step):
        tokens = pl.ds(step * chunk, chunk)
        left = ga[tokens].reshape(chunk * half, -1)
        right = ha[tokens].reshape(chunk * half, -1)
        acc[...] += lax.dot_general(
            left, right, (((0,), (0,)), ((), ())), preferred_element_type=F32
        )

    def to_sibling(src, dst, key):
        return pltpu.make_async_remote_copy(
            src_ref=src,
            dst_ref=dst,
            send_sem=d_send.at[key],
            recv_sem=d_recv.at[key],
            device_id=sibling,
            device_id_type=MESH,
        )

    weight_swap = to_sibling(acc, acc_in, 0)
    start(weight_swap)
    weight_swap.wait_recv()
    gw_ref[...] = (acc[...] + acc_in[...]).astype(BF16)

    for part in (0, 1):
        rows = pl.ds(part * quarter, quarter)
        value = total(y, rows)
        for sign, _, far, key, which in plans:
            if which == part:
                for last in (key + 1, key + 3 if far == 4 else key + 2):
                    along(last, y).wait_recv()
                    value += yr[last].astype(F32)
        half_s[rows] = value.astype(BF16)
    half_swap = to_sibling(half_s, half_r, 1)
    start(half_swap)
    gh_ref[mine] = half_s[...]
    half_swap.wait_recv()
    gh_ref[pl.ds(pl.multiple_of((1 - depth) * half, half), half)] = half_r[...]
    for copy in sent:
        copy.wait_send()
    @pl.when(lane != grad.lane)
    def _():
        for copy in third:
            copy.wait_send()


def body(grad_out, hidden, weight):
    (tokens, features), units = grad_out.shape, hidden.shape[1]
    half, quarter, blocks = tokens // 2, tokens // 4, 2 * RING
    dma = pltpu.SemaphoreType.DMA
    vmem = pl.BlockSpec(memory_space=pltpu.VMEM)
    grads = len(GRAD_HOPS) + 3
    hiddens = len(HIDDEN_HOPS) + 1 + len(HANDED)
    return pl.pallas_call(
        kernel,
        out_shape=(
            jax.ShapeDtypeStruct(hidden.shape, BF16),
            jax.ShapeDtypeStruct(weight.shape, BF16),
        ),
        in_specs=[vmem] * 3,
        out_specs=(vmem, vmem),
        scratch_shapes=[
            pltpu.VMEM((blocks + RING, half, features), BF16),
            pltpu.VMEM((blocks, half, units), BF16),
            pltpu.VMEM(weight.shape, BF16),
            pltpu.VMEM((RING, half, units), F32),
            pltpu.VMEM((14, quarter, units), BF16),
            pltpu.VMEM((14, quarter, units), BF16),
            pltpu.VMEM((features, units), F32),
            pltpu.VMEM((features, units), F32),
            pltpu.VMEM((half, units), BF16),
            pltpu.VMEM((half, units), BF16),
            dma((grads,)), dma((grads,)), dma((hiddens,)), dma((hiddens,)),
            dma((2,)), dma((2,)), dma((14,)), dma((14,)), dma((2,)), dma((2,)),
        ],
        compiler_params=pltpu.CompilerParams(
            collective_id=0, has_side_effects=True, vmem_limit_bytes=56 << 20
        ),
    )(grad_out, hidden, weight)


def solution(mesh):
    return jax.shard_map(
        body,
        mesh=mesh,
        in_specs=(P("col", "row"), P("row", "col"), P("row", "col")),
        out_specs=(P("row", "col"), P("row", "col")),
        check_vma=False,
    )
```

```python
import jax
import jax.numpy as jnp
from jax import lax
from jax.experimental import pallas as pl
from jax.experimental.pallas import tpu as pltpu
from jax.sharding import PartitionSpec as P

MESH = pl.DeviceIdType.MESH
BF16, F32 = jnp.bfloat16, jnp.float32
RING = 8
GRAD_HOPS = [
    (sign, lane, hop)
    for hop in (1, 2, 3, 4)
    for lane in (0, 1, 2)
    for sign in (1, -1)
    if hop < 4 or (sign == 1) == (lane != 1)
]
HIDDEN_HOPS = [(1, 0, 1), (-1, 0, 1), (1, 0, 2), (-1, 0, 2), (1, 0, 3), (-1, 0, 3), (1, 0, 4)]
HIDDEN_HOPS += [(1, 1, 1), (-1, 1, 1), (-1, 1, 2)]
HANDED = [(1, 0, 2), (1, 0, 3), (-1, 0, 3), (1, 0, 4)]


def wrap(pos):
    return lax.rem(pos + RING, RING)


class Gather:
    def __init__(self, axis, hops, own, full, send, recv):
        at = lax.axis_index(axis)
        self.axis, self.hops, self.own, self.full = axis, hops, own, full
        self.send, self.recv = send, recv
        self.pos, self.lane = at // 2, lax.rem(at, 2)

    def device(self, pos, lane):
        return {self.axis: wrap(pos) * 2 + lane}

    def slot(self, pos, lane):
        if lane == 2:
            return 2 * RING + wrap(pos)
        return wrap(pos) * 2 + (1 - self.lane if lane else self.lane)

    def copy(self, src, slot, key, device):
        return pltpu.make_async_remote_copy(
            src_ref=src,
            dst_ref=self.full.at[slot],
            send_sem=self.send.at[key],
            recv_sem=self.recv.at[key],
            device_id=device,
            device_id_type=MESH,
        )

    def partner(self):
        return self.device(self.pos, 1 - self.lane)

    def swap(self):
        return self.copy(self.own, self.slot(self.pos, 0), len(self.hops), self.partner())

    def swapped(self):
        slot = self.slot(self.pos, 1)
        self.copy(self.full.at[slot], slot, len(self.hops), self.partner()).wait_recv()

    def hop(self, sign, lane, hop):
        slot = self.slot(self.pos - sign * (hop - 1), lane)
        src = self.own if hop == 1 and not lane else self.full.at[slot]
        key = self.hops.index((sign, lane, hop))
        return self.copy(src, slot, key, self.device(self.pos + sign, self.lane))

    def arrived(self, sign, lane, hop):
        slot = self.slot(self.pos - sign * hop, lane)
        key = self.hops.index((sign, lane, hop))
        device = self.device(self.pos - sign, self.lane)
        self.copy(self.full.at[slot], slot, key, device).wait_recv()

    def hand(self, index):
        sign, _, hop = HANDED[index]
        slot = self.slot(self.pos - sign * hop, 0)
        return self.copy(self.full.at[slot], slot, len(self.hops) + 1 + index, self.partner())

    def handed(self, index):
        sign, _, hop = HANDED[index]
        slot = self.slot(self.pos - sign * hop, 1)
        key = len(self.hops) + 1 + index
        self.copy(self.full.at[slot], slot, key, self.partner()).wait_recv()


def kernel(
    g_ref, h_ref, w_ref, gh_ref, gw_ref,
    ga, ha, wo, kept, ys, yr, acc, acc_in, half_s, half_r,
    g_send, g_recv, h_send, h_recv, w_send, w_recv, y_send, y_recv, d_send, d_recv,
):
    depth = lax.axis_index("depth")
    half = g_ref.shape[0] // 2
    quarter = half // 2
    mine = pl.ds(pl.multiple_of(depth * half, half), half)
    grad = Gather("col", GRAD_HOPS, g_ref.at[mine], ga, g_send, g_recv)
    hidden = Gather("row", HIDDEN_HOPS, h_ref.at[mine], ha, h_send, h_recv)
    y, lane = hidden.pos, hidden.lane

    def row_device(pos):
        return {"row": wrap(pos) * 2 + lane}

    partner = hidden.partner()
    sibling = {"depth": 1 - depth}
    across = partner | grad.partner()

    barrier = pltpu.get_barrier_semaphore()
    peers = [partner, sibling, across, grad.partner()]
    peers += [grad.device(grad.pos + k, grad.lane) for k in (-1, 1)]
    peers += [row_device(y + k) for k in (-3, -2, -1, 1, 2, 3)]
    for peer in peers:
        pl.semaphore_signal(barrier, inc=1, device_id=peer, device_id_type=MESH)
    pl.semaphore_wait(barrier, len(peers))

    sent = []

    def start(copy):
        copy.start()
        sent.append(copy)

    lane_2 = len(GRAD_HOPS) + 1
    third = [grad.copy(grad.own, grad.slot(grad.pos, 2), lane_2 + i, to) for i, to in enumerate((partner, across))]

    def third_arrived():
        slot = grad.slot(grad.pos, 2)
        for i, (source, here) in enumerate(((partner, lane == grad.lane), (across, lane != grad.lane))):
            @pl.when(here)
            def _():
                grad.copy(ga.at[slot], slot, lane_2 + i, source).wait_recv()

    features = w_ref.shape[0] // 2
    part = pl.ds(pl.multiple_of(depth * features, features), features)
    rest = pl.ds(pl.multiple_of((1 - depth) * features, features), features)

    def weights(src, rows, key, device):
        return pltpu.make_async_remote_copy(
            src_ref=src.at[rows],
            dst_ref=wo.at[rows],
            send_sem=w_send.at[key],
            recv_sem=w_recv.at[key],
            device_id=device,
            device_id_type=MESH,
        )

    for sign in (1, -1):
        start(grad.hop(sign, 0, 1))
    @pl.when(lane != grad.lane)
    def _():
        for copy in third:
            copy.start()
    start(grad.swap())
    for sign in (1, -1):
        start(hidden.hop(sign, 0, 1))
    start(weights(w_ref, part, 0, partner))
    start(hidden.swap())
    for gather in (grad, hidden):
        gather.full[gather.slot(gather.pos, 0)] = gather.own[...]

    def hidden_round(lane, hop):
        for key in HIDDEN_HOPS:
            if key[1:] == (lane, hop):
                hidden.arrived(*key)
                following = (*key[:2], hop + 1)
                if following in HIDDEN_HOPS:
                    start(hidden.hop(*following))
                if key in HANDED:
                    start(hidden.hand(HANDED.index(key)))

    def product(pos):
        pos = wrap(pos)
        value = jnp.dot(ga[pos * 2 + lane], w_ref[...], preferred_element_type=F32)
        kept[pos] = value + jnp.dot(ga[2 * RING + pos], wo[...], preferred_element_type=F32)

    def total(pos, rows):
        return kept[wrap(pos), rows]

    plans, singles, sums, at = [], [], [], 0
    for sign in (1, -1):
        for piece in (0, 1):
            far = 4 if (piece == 0) == (sign == 1) else 3
            rows = pl.ds(piece * quarter, quarter)
            plans.append((far, at, piece))
            singles.append((sign * far % RING, at, rows, sign))
            sums.append((sign * (far - 1) % RING, at, at + 1, rows, sign * (far - 1)))
            if far == 4:
                singles.append((sign * 2 % RING, at + 2, rows, sign))
                sums.append((sign % RING, at + 2, at + 3, rows, sign))
            else:
                singles.append((sign % RING, at + 2, rows, sign))
            at += far
    messages = at

    def along(key, pos):
        return pltpu.make_async_remote_copy(
            src_ref=ys.at[key],
            dst_ref=yr.at[key],
            send_sem=y_send.at[key],
            recv_sem=y_recv.at[key],
            device_id=row_device(pos),
            device_id_type=MESH,
        )

    def emit(key, value, pos):
        ys[key] = value.astype(BF16)
        along(key, pos).start()

    def near_and_far(hop):
        return [grad.pos - hop] + ([grad.pos + hop] if 0 < hop < 4 else [])

    def send_singles(hop):
        for pos in near_and_far(hop):
            product(pos)
            place = lax.rem(wrap(pos) - y + RING, RING)
            for when in range(1, RING):
                @pl.when(place == when)
                def _():
                    for target, key, rows, to in singles:
                        if target == when:
                            emit(key, total(pos, rows), y + to)

    def send_sums(hop):
        for pos in near_and_far(hop):
            place = lax.rem(wrap(pos) - y + RING, RING)
            for when in range(1, RING):
                @pl.when(place == when)
                def _():
                    for target, source, key, rows, to in sums:
                        if target == when:
                            along(source, y).wait_recv()
                            emit(key, total(pos, rows) + yr[source].astype(F32), y + to)

    def grad_lane(lane, hop):
        for key in GRAD_HOPS:
            if key[1:] == (lane, hop):
                grad.arrived(*key)
                following = (*key[:2], hop + 1)
                if following in GRAD_HOPS:
                    start(grad.hop(*following))

    grad_lane(0, 1)
    third_arrived()
    for sign in (1, -1):
        start(grad.hop(sign, 2, 1))
    grad.swapped()
    for sign in (1, -1):
        start(grad.hop(sign, 1, 1))
    hidden_round(0, 1)
    weights(w_ref, part, 0, partner).wait_recv()
    start(weights(wo, part, 1, sibling))
    hidden_round(0, 2)
    hidden.swapped()
    for sign in (1, -1):
        start(hidden.hop(sign, 1, 1))
    for which in (1, 2):
        grad_lane(which, 1)
    weights(wo, rest, 1, sibling).wait_recv()
    send_singles(0)
    send_singles(1)
    hidden_round(0, 3)
    for which in (0, 1, 2):
        grad_lane(which, 2)
    send_sums(0)
    send_sums(1)
    send_singles(2)
    hidden_round(1, 1)
    for which in (0, 1, 2):
        grad_lane(which, 3)
    send_sums(2)
    send_singles(3)
    hidden_round(0, 4)
    for which in (0, 1, 2):
        grad_lane(which, 4)
    send_singles(4)
    send_sums(3)
    send_sums(4)

    hidden_round(1, 2)
    for index in range(len(HANDED)):
        hidden.handed(index)
    acc[...] = jnp.zeros_like(acc)
    chunk = 4

    @pl.loop(0, 2 * RING // chunk)
    def _(step):
        tokens = pl.ds(step * chunk, chunk)
        left = ga[tokens].reshape(chunk * half, -1)
        right = ha[tokens].reshape(chunk * half, -1)
        acc[...] += lax.dot_general(
            left, right, (((0,), (0,)), ((), ())), preferred_element_type=F32
        )

    def to_sibling(src, dst, key):
        return pltpu.make_async_remote_copy(
            src_ref=src,
            dst_ref=dst,
            send_sem=d_send.at[key],
            recv_sem=d_recv.at[key],
            device_id=sibling,
            device_id_type=MESH,
        )

    weight_swap = to_sibling(acc, acc_in, 0)
    start(weight_swap)
    weight_swap.wait_recv()
    gw_ref[...] = (acc[...] + acc_in[...]).astype(BF16)

    for part in (0, 1):
        rows = pl.ds(part * quarter, quarter)
        value = total(y, rows)
        for far, key, which in plans:
            if which == part:
                for last in (key + 1, key + 3 if far == 4 else key + 2):
                    along(last, y).wait_recv()
                    value += yr[last].astype(F32)
        half_s[rows] = value.astype(BF16)
    half_swap = to_sibling(half_s, half_r, 1)
    start(half_swap)
    gh_ref[mine] = half_s[...]
    half_swap.wait_recv()
    gh_ref[pl.ds(pl.multiple_of((1 - depth) * half, half), half)] = half_r[...]
    for copy in sent:
        copy.wait_send()
    for key in range(messages):
        along(key, y).wait_send()
    @pl.when(lane != grad.lane)
    def _():
        for copy in third:
            copy.wait_send()


def body(grad_out, hidden, weight):
    (tokens, features), units = grad_out.shape, hidden.shape[1]
    half, quarter, blocks = tokens // 2, tokens // 4, 2 * RING
    dma = pltpu.SemaphoreType.DMA
    vmem = pl.BlockSpec(memory_space=pltpu.VMEM)
    grads = len(GRAD_HOPS) + 3
    hiddens = len(HIDDEN_HOPS) + 1 + len(HANDED)
    return pl.pallas_call(
        kernel,
        out_shape=(
            jax.ShapeDtypeStruct(hidden.shape, BF16),
            jax.ShapeDtypeStruct(weight.shape, BF16),
        ),
        in_specs=[vmem] * 3,
        out_specs=(vmem, vmem),
        scratch_shapes=[
            pltpu.VMEM((blocks + RING, half, features), BF16),
            pltpu.VMEM((blocks, half, units), BF16),
            pltpu.VMEM(weight.shape, BF16),
            pltpu.VMEM((RING, half, units), F32),
            pltpu.VMEM((14, quarter, units), BF16),
            pltpu.VMEM((14, quarter, units), BF16),
            pltpu.VMEM((features, units), F32),
            pltpu.VMEM((features, units), F32),
            pltpu.VMEM((half, units), BF16),
            pltpu.VMEM((half, units), BF16),
            dma((grads,)), dma((grads,)), dma((hiddens,)), dma((hiddens,)),
            dma((2,)), dma((2,)), dma((14,)), dma((14,)), dma((2,)), dma((2,)),
        ],
        compiler_params=pltpu.CompilerParams(
            collective_id=0, has_side_effects=True, vmem_limit_bytes=56 << 20
        ),
    )(grad_out, hidden, weight)


def solution(mesh):
    return jax.shard_map(
        body,
        mesh=mesh,
        in_specs=(P("col", "row"), P("row", "col"), P("row", "col")),
        out_specs=(P("row", "col"), P("row", "col")),
        check_vma=False,
    )
```

```python
import jax
import jax.numpy as jnp
from jax import lax
from jax.experimental import pallas as pl
from jax.experimental.pallas import tpu as pltpu
from jax.sharding import PartitionSpec as P

MESH = pl.DeviceIdType.MESH
BF16, F32 = jnp.bfloat16, jnp.float32
RING = 8
GRAD_HOPS = [
    (sign, lane, hop)
    for hop in (1, 2, 3, 4)
    for lane in (0, 1, 2)
    for sign in (1, -1)
    if hop < 4 or (sign == 1) == (lane != 1)
]
HIDDEN_HOPS = [(1, 0, 1), (-1, 0, 1), (1, 0, 2), (-1, 0, 2), (1, 0, 3), (-1, 0, 3), (1, 0, 4)]
HIDDEN_HOPS += [(1, 1, 1), (-1, 1, 1), (-1, 1, 2)]
HANDED = [(1, 0, 2), (1, 0, 3), (-1, 0, 3), (1, 0, 4)]


def wrap(pos):
    return lax.rem(pos + RING, RING)


class Gather:
    def __init__(self, axis, hops, own, full, send, recv):
        at = lax.axis_index(axis)
        self.axis, self.hops, self.own, self.full = axis, hops, own, full
        self.send, self.recv = send, recv
        self.pos, self.lane = at // 2, lax.rem(at, 2)

    def device(self, pos, lane):
        return {self.axis: wrap(pos) * 2 + lane}

    def slot(self, pos, lane):
        if lane == 2:
            return 2 * RING + wrap(pos)
        return wrap(pos) * 2 + (1 - self.lane if lane else self.lane)

    def copy(self, src, slot, key, device):
        return pltpu.make_async_remote_copy(
            src_ref=src,
            dst_ref=self.full.at[slot],
            send_sem=self.send.at[key],
            recv_sem=self.recv.at[key],
            device_id=device,
            device_id_type=MESH,
        )

    def partner(self):
        return self.device(self.pos, 1 - self.lane)

    def swap(self):
        return self.copy(self.own, self.slot(self.pos, 0), len(self.hops), self.partner())

    def swapped(self):
        slot = self.slot(self.pos, 1)
        self.copy(self.full.at[slot], slot, len(self.hops), self.partner()).wait_recv()

    def hop(self, sign, lane, hop):
        slot = self.slot(self.pos - sign * (hop - 1), lane)
        src = self.own if hop == 1 and not lane else self.full.at[slot]
        key = self.hops.index((sign, lane, hop))
        return self.copy(src, slot, key, self.device(self.pos + sign, self.lane))

    def arrived(self, sign, lane, hop):
        slot = self.slot(self.pos - sign * hop, lane)
        key = self.hops.index((sign, lane, hop))
        device = self.device(self.pos - sign, self.lane)
        self.copy(self.full.at[slot], slot, key, device).wait_recv()

    def hand(self, index):
        sign, _, hop = HANDED[index]
        slot = self.slot(self.pos - sign * hop, 0)
        return self.copy(self.full.at[slot], slot, len(self.hops) + 1 + index, self.partner())

    def handed(self, index):
        sign, _, hop = HANDED[index]
        slot = self.slot(self.pos - sign * hop, 1)
        key = len(self.hops) + 1 + index
        self.copy(self.full.at[slot], slot, key, self.partner()).wait_recv()


def kernel(
    g_ref, h_ref, w_ref, gh_ref, gw_ref,
    ga, ha, wo, kept, ys, yr, acc, acc_in, half_s, half_r,
    g_send, g_recv, h_send, h_recv, w_send, w_recv, y_send, y_recv, d_send, d_recv,
):
    depth = lax.axis_index("depth")
    half = g_ref.shape[0] // 2
    quarter = half // 2
    mine = pl.ds(pl.multiple_of(depth * half, half), half)
    grad = Gather("col", GRAD_HOPS, g_ref.at[mine], ga, g_send, g_recv)
    hidden = Gather("row", HIDDEN_HOPS, h_ref.at[mine], ha, h_send, h_recv)
    y, lane = hidden.pos, hidden.lane

    def row_device(pos):
        return {"row": wrap(pos) * 2 + lane}

    partner = hidden.partner()
    sibling = {"depth": 1 - depth}
    across = partner | grad.partner()

    barrier = pltpu.get_barrier_semaphore()
    peers = [partner, sibling, across, grad.partner()]
    peers += [grad.device(grad.pos + k, grad.lane) for k in (-1, 1)]
    peers += [row_device(y + k) for k in (-3, -2, -1, 1, 2, 3)]
    for peer in peers:
        pl.semaphore_signal(barrier, inc=1, device_id=peer, device_id_type=MESH)
    pl.semaphore_wait(barrier, len(peers))

    sent = []

    def start(copy):
        copy.start()
        sent.append(copy)

    lane_2 = len(GRAD_HOPS) + 1
    third = [grad.copy(grad.own, grad.slot(grad.pos, 2), lane_2 + i, to) for i, to in enumerate((partner, across))]

    def third_arrived():
        slot = grad.slot(grad.pos, 2)
        for i, (source, here) in enumerate(((partner, lane == grad.lane), (across, lane != grad.lane))):
            @pl.when(here)
            def _():
                grad.copy(ga.at[slot], slot, lane_2 + i, source).wait_recv()

    features = w_ref.shape[0] // 2
    part = pl.ds(pl.multiple_of(depth * features, features), features)
    rest = pl.ds(pl.multiple_of((1 - depth) * features, features), features)

    def weights(src, rows, key, device):
        return pltpu.make_async_remote_copy(
            src_ref=src.at[rows],
            dst_ref=wo.at[rows],
            send_sem=w_send.at[key],
            recv_sem=w_recv.at[key],
            device_id=device,
            device_id_type=MESH,
        )

    for sign in (1, -1):
        start(grad.hop(sign, 0, 1))
    @pl.when(lane != grad.lane)
    def _():
        for copy in third:
            copy.start()
    start(grad.swap())
    for sign in (1, -1):
        start(hidden.hop(sign, 0, 1))
    start(weights(w_ref, part, 0, partner))
    start(hidden.swap())
    for gather in (grad, hidden):
        gather.full[gather.slot(gather.pos, 0)] = gather.own[...]

    def hidden_round(lane, hop):
        for key in HIDDEN_HOPS:
            if key[1:] == (lane, hop):
                hidden.arrived(*key)
                following = (*key[:2], hop + 1)
                if following in HIDDEN_HOPS:
                    start(hidden.hop(*following))
                if key in HANDED:
                    start(hidden.hand(HANDED.index(key)))

    def product(pos):
        pos = wrap(pos)
        value = jnp.dot(ga[pos * 2 + lane], w_ref[...], preferred_element_type=F32)
        kept[pos] = value + jnp.dot(ga[2 * RING + pos], wo[...], preferred_element_type=F32)

    def total(pos, rows):
        return kept[wrap(pos), rows]

    plans, singles, sums, at = [], [], [], 0
    for sign in (1, -1):
        for piece in (0, 1):
            far = 4 if (piece == 0) == (sign == 1) else 3
            rows = pl.ds(piece * quarter, quarter)
            plans.append((far, at, piece))
            singles.append((sign * far % RING, at, rows, sign))
            sums.append((sign * (far - 1) % RING, at, at + 1, rows, sign * (far - 1)))
            if far == 4:
                singles.append((sign * 2 % RING, at + 2, rows, sign))
                sums.append((sign % RING, at + 2, at + 3, rows, sign))
            else:
                singles.append((sign % RING, at + 2, rows, sign))
            at += far
    messages = at

    def along(key, pos):
        return pltpu.make_async_remote_copy(
            src_ref=ys.at[key],
            dst_ref=yr.at[key],
            send_sem=y_send.at[key],
            recv_sem=y_recv.at[key],
            device_id=row_device(pos),
            device_id_type=MESH,
        )

    def emit(key, value, pos):
        ys[key] = value.astype(BF16)
        along(key, pos).start()

    def near_and_far(hop):
        return [grad.pos - hop] + ([grad.pos + hop] if 0 < hop < 4 else [])

    def send_singles(hop):
        for pos in near_and_far(hop):
            product(pos)
            place = lax.rem(wrap(pos) - y + RING, RING)
            for when in range(1, RING):
                @pl.when(place == when)
                def _():
                    for target, key, rows, to in singles:
                        if target == when:
                            emit(key, total(pos, rows), y + to)

    def send_sums(hop):
        for pos in near_and_far(hop):
            place = lax.rem(wrap(pos) - y + RING, RING)
            for when in range(1, RING):
                @pl.when(place == when)
                def _():
                    for target, source, key, rows, to in sums:
                        if target == when:
                            along(source, y).wait_recv()
                            emit(key, total(pos, rows) + yr[source].astype(F32), y + to)

    def grad_lane(lane, hop):
        for key in GRAD_HOPS:
            if key[1:] == (lane, hop):
                grad.arrived(*key)
                following = (*key[:2], hop + 1)
                if following in GRAD_HOPS:
                    start(grad.hop(*following))

    grad_lane(0, 1)
    third_arrived()
    for sign in (1, -1):
        start(grad.hop(sign, 2, 1))
    grad.swapped()
    for sign in (1, -1):
        start(grad.hop(sign, 1, 1))
    hidden_round(0, 1)
    grad_lane(0, 2)
    grad_lane(2, 1)
    grad_lane(1, 1)
    hidden_round(0, 2)
    grad_lane(0, 3)
    grad_lane(2, 2)
    grad_lane(1, 2)
    weights(w_ref, part, 0, partner).wait_recv()
    start(weights(wo, part, 1, sibling))
    hidden_round(0, 3)
    grad_lane(2, 3)
    grad_lane(1, 3)
    weights(wo, rest, 1, sibling).wait_recv()
    send_singles(0)
    send_singles(1)
    hidden.swapped()
    for sign in (1, -1):
        start(hidden.hop(sign, 1, 1))
    send_singles(2)
    hidden_round(0, 4)
    send_singles(3)
    for which in (0, 2, 1):
        grad_lane(which, 4)
    send_singles(4)
    for hop in range(5):
        send_sums(hop)
    hidden_round(1, 1)

    hidden_round(1, 2)
    for index in range(len(HANDED)):
        hidden.handed(index)
    acc[...] = jnp.zeros_like(acc)
    chunk = 4

    @pl.loop(0, 2 * RING // chunk)
    def _(step):
        tokens = pl.ds(step * chunk, chunk)
        left = ga[tokens].reshape(chunk * half, -1)
        right = ha[tokens].reshape(chunk * half, -1)
        acc[...] += lax.dot_general(
            left, right, (((0,), (0,)), ((), ())), preferred_element_type=F32
        )

    def to_sibling(src, dst, key):
        return pltpu.make_async_remote_copy(
            src_ref=src,
            dst_ref=dst,
            send_sem=d_send.at[key],
            recv_sem=d_recv.at[key],
            device_id=sibling,
            device_id_type=MESH,
        )

    weight_swap = to_sibling(acc, acc_in, 0)
    start(weight_swap)
    weight_swap.wait_recv()
    gw_ref[...] = (acc[...] + acc_in[...]).astype(BF16)

    for part in (0, 1):
        rows = pl.ds(part * quarter, quarter)
        value = total(y, rows)
        for far, key, which in plans:
            if which == part:
                for last in (key + 1, key + 3 if far == 4 else key + 2):
                    along(last, y).wait_recv()
                    value += yr[last].astype(F32)
        half_s[rows] = value.astype(BF16)
    half_swap = to_sibling(half_s, half_r, 1)
    start(half_swap)
    gh_ref[mine] = half_s[...]
    half_swap.wait_recv()
    gh_ref[pl.ds(pl.multiple_of((1 - depth) * half, half), half)] = half_r[...]
    for copy in sent:
        copy.wait_send()
    for key in range(messages):
        along(key, y).wait_send()
    @pl.when(lane != grad.lane)
    def _():
        for copy in third:
            copy.wait_send()


def body(grad_out, hidden, weight):
    (tokens, features), units = grad_out.shape, hidden.shape[1]
    half, quarter, blocks = tokens // 2, tokens // 4, 2 * RING
    dma = pltpu.SemaphoreType.DMA
    vmem = pl.BlockSpec(memory_space=pltpu.VMEM)
    grads = len(GRAD_HOPS) + 3
    hiddens = len(HIDDEN_HOPS) + 1 + len(HANDED)
    return pl.pallas_call(
        kernel,
        out_shape=(
            jax.ShapeDtypeStruct(hidden.shape, BF16),
            jax.ShapeDtypeStruct(weight.shape, BF16),
        ),
        in_specs=[vmem] * 3,
        out_specs=(vmem, vmem),
        scratch_shapes=[
            pltpu.VMEM((blocks + RING, half, features), BF16),
            pltpu.VMEM((blocks, half, units), BF16),
            pltpu.VMEM(weight.shape, BF16),
            pltpu.VMEM((RING, half, units), F32),
            pltpu.VMEM((14, quarter, units), BF16),
            pltpu.VMEM((14, quarter, units), BF16),
            pltpu.VMEM((features, units), F32),
            pltpu.VMEM((features, units), F32),
            pltpu.VMEM((half, units), BF16),
            pltpu.VMEM((half, units), BF16),
            dma((grads,)), dma((grads,)), dma((hiddens,)), dma((hiddens,)),
            dma((2,)), dma((2,)), dma((14,)), dma((14,)), dma((2,)), dma((2,)),
        ],
        compiler_params=pltpu.CompilerParams(
            collective_id=0, has_side_effects=True, vmem_limit_bytes=56 << 20
        ),
    )(grad_out, hidden, weight)


def solution(mesh):
    return jax.shard_map(
        body,
        mesh=mesh,
        in_specs=(P("col", "row"), P("row", "col"), P("row", "col")),
        out_specs=(P("row", "col"), P("row", "col")),
        check_vma=False,
    )
```

```python
import jax
import jax.numpy as jnp
from jax import lax
from jax.experimental import pallas as pl
from jax.experimental.pallas import tpu as pltpu
from jax.sharding import PartitionSpec as P

MESH = pl.DeviceIdType.MESH
BF16, F32 = jnp.bfloat16, jnp.float32
RING = 8
GRAD_HOPS = [
    (sign, lane, hop)
    for hop in (1, 2, 3, 4)
    for lane in (0, 1, 2)
    for sign in (1, -1)
    if ((sign, hop) in ((1, 1), (-1, 1), (-1, 2)) if lane == 2 else hop < 4 or (sign == 1) == (lane == 0))
]
THIRDS = [(1, 0, 2), (1, 0, 3), (-1, 0, 3), (1, 0, 4)]
HIDDEN_HOPS = [(1, 0, 1), (-1, 0, 1), (1, 0, 2), (-1, 0, 2), (1, 0, 3), (-1, 0, 3), (1, 0, 4)]
HIDDEN_HOPS += [(1, 1, 1), (-1, 1, 1), (1, 1, 2), (-1, 1, 2)]
HANDED = [(1, 0, 3), (-1, 0, 3), (1, 0, 4)]


def wrap(pos):
    return lax.rem(pos + RING, RING)


class Gather:
    def __init__(self, axis, hops, own, full, send, recv):
        at = lax.axis_index(axis)
        self.axis, self.hops, self.own, self.full = axis, hops, own, full
        self.send, self.recv = send, recv
        self.pos, self.lane = at // 2, lax.rem(at, 2)

    def device(self, pos, lane):
        return {self.axis: wrap(pos) * 2 + lane}

    def slot(self, pos, lane):
        if lane == 2:
            return 2 * RING + wrap(pos)
        return wrap(pos) * 2 + (1 - self.lane if lane else self.lane)

    def copy(self, src, slot, key, device):
        return pltpu.make_async_remote_copy(
            src_ref=src,
            dst_ref=self.full.at[slot],
            send_sem=self.send.at[key],
            recv_sem=self.recv.at[key],
            device_id=device,
            device_id_type=MESH,
        )

    def partner(self):
        return self.device(self.pos, 1 - self.lane)

    def swap(self):
        return self.copy(self.own, self.slot(self.pos, 0), len(self.hops), self.partner())

    def swapped(self):
        slot = self.slot(self.pos, 1)
        self.copy(self.full.at[slot], slot, len(self.hops), self.partner()).wait_recv()

    def hop(self, sign, lane, hop):
        slot = self.slot(self.pos - sign * (hop - 1), lane)
        src = self.own if hop == 1 and not lane else self.full.at[slot]
        key = self.hops.index((sign, lane, hop))
        return self.copy(src, slot, key, self.device(self.pos + sign, self.lane))

    def arrived(self, sign, lane, hop):
        slot = self.slot(self.pos - sign * hop, lane)
        key = self.hops.index((sign, lane, hop))
        device = self.device(self.pos - sign, self.lane)
        self.copy(self.full.at[slot], slot, key, device).wait_recv()

    def hand(self, index):
        sign, _, hop = HANDED[index]
        slot = self.slot(self.pos - sign * hop, 0)
        return self.copy(self.full.at[slot], slot, len(self.hops) + 1 + index, self.partner())

    def handed(self, index):
        sign, _, hop = HANDED[index]
        slot = self.slot(self.pos - sign * hop, 1)
        key = len(self.hops) + 1 + index
        self.copy(self.full.at[slot], slot, key, self.partner()).wait_recv()


def kernel(
    g_ref, h_ref, w_ref, gh_ref, gw_ref,
    ga, ha, wo, kept, ys, yr, acc, acc_in, half_s, half_r,
    g_send, g_recv, h_send, h_recv, w_send, w_recv, y_send, y_recv, d_send, d_recv,
):
    depth = lax.axis_index("depth")
    half = g_ref.shape[0] // 2
    quarter = half // 2
    mine = pl.ds(pl.multiple_of(depth * half, half), half)
    grad = Gather("col", GRAD_HOPS, g_ref.at[mine], ga, g_send, g_recv)
    hidden = Gather("row", HIDDEN_HOPS, h_ref.at[mine], ha, h_send, h_recv)
    y, lane = hidden.pos, hidden.lane

    def row_device(pos):
        return {"row": wrap(pos) * 2 + lane}

    partner = hidden.partner()
    sibling = {"depth": 1 - depth}
    across = partner | grad.partner()

    barrier = pltpu.get_barrier_semaphore()
    peers = [partner, sibling, across, grad.partner()]
    peers += [grad.device(grad.pos + k, grad.lane) for k in (-1, 1)]
    peers += [row_device(y + k) for k in (-3, -2, -1, 1, 2, 3)]
    for peer in peers:
        pl.semaphore_signal(barrier, inc=1, device_id=peer, device_id_type=MESH)
    pl.semaphore_wait(barrier, len(peers))

    sent = []

    def start(copy):
        copy.start()
        sent.append(copy)

    lane_2 = len(GRAD_HOPS) + 1
    def thirds(index):
        if index == len(THIRDS):
            pos, src = grad.pos, grad.own
        else:
            sign, _, hop = THIRDS[index]
            pos = grad.pos - sign * hop
            src = ga.at[grad.slot(pos, 0)]
        slot, key = grad.slot(pos, 2), lane_2 + 2 * index
        return [grad.copy(src, slot, key + i, to) for i, to in enumerate((partner, across))]

    def send_thirds(index):
        @pl.when(lane != grad.lane)
        def _():
            for copy in thirds(index):
                copy.start()

    def third_arrived(index):
        @pl.when(lane == grad.lane)
        def _():
            thirds(index)[0].wait_recv()
        @pl.when(lane != grad.lane)
        def _():
            thirds(index)[1].wait_recv()

    features = w_ref.shape[0] // 2
    part = pl.ds(pl.multiple_of(depth * features, features), features)
    rest = pl.ds(pl.multiple_of((1 - depth) * features, features), features)

    def weights(src, rows, key, device):
        return pltpu.make_async_remote_copy(
            src_ref=src.at[rows],
            dst_ref=wo.at[rows],
            send_sem=w_send.at[key],
            recv_sem=w_recv.at[key],
            device_id=device,
            device_id_type=MESH,
        )

    for sign in (1, -1):
        start(grad.hop(sign, 0, 1))
    send_thirds(len(THIRDS))
    start(grad.swap())
    for sign in (1, -1):
        start(hidden.hop(sign, 0, 1))
    start(weights(w_ref, part, 0, partner))
    start(hidden.swap())
    for gather in (grad, hidden):
        gather.full[gather.slot(gather.pos, 0)] = gather.own[...]

    def hidden_round(lane, hop):
        for key in HIDDEN_HOPS:
            if key[1:] == (lane, hop):
                hidden.arrived(*key)
                following = (*key[:2], hop + 1)
                if following in HIDDEN_HOPS:
                    start(hidden.hop(*following))

    def product(pos):
        pos = wrap(pos)
        value = jnp.dot(ga[pos * 2 + lane], w_ref[...], preferred_element_type=F32)
        kept[pos] = value + jnp.dot(ga[2 * RING + pos], wo[...], preferred_element_type=F32)

    def total(pos, rows):
        return kept[wrap(pos), rows]

    plans, singles, sums, at = [], [], [], 0
    for sign in (1, -1):
        for piece in (0, 1):
            far = 4 if (piece == 0) == (sign == 1) else 3
            rows = pl.ds(piece * quarter, quarter)
            plans.append((far, at, piece))
            singles.append((sign * far % RING, at, rows, sign))
            sums.append((sign * (far - 1) % RING, at, at + 1, rows, sign * (far - 1)))
            if far == 4:
                singles.append((sign * 2 % RING, at + 2, rows, sign))
                sums.append((sign % RING, at + 2, at + 3, rows, sign))
            else:
                singles.append((sign % RING, at + 2, rows, sign))
            at += far
    messages = at

    def along(key, pos):
        return pltpu.make_async_remote_copy(
            src_ref=ys.at[key],
            dst_ref=yr.at[key],
            send_sem=y_send.at[key],
            recv_sem=y_recv.at[key],
            device_id=row_device(pos),
            device_id_type=MESH,
        )

    def emit(key, value, pos):
        ys[key] = value.astype(BF16)
        along(key, pos).start()

    def near_and_far(hop):
        return [grad.pos - hop] + ([grad.pos + hop] if 0 < hop < 4 else [])

    def send_singles(hop):
        for pos in near_and_far(hop):
            product(pos)
            place = lax.rem(wrap(pos) - y + RING, RING)
            for when in range(1, RING):
                @pl.when(place == when)
                def _():
                    for target, key, rows, to in singles:
                        if target == when:
                            emit(key, total(pos, rows), y + to)

    def send_sums(hop):
        for pos in near_and_far(hop):
            place = lax.rem(wrap(pos) - y + RING, RING)
            for when in range(1, RING):
                @pl.when(place == when)
                def _():
                    for target, source, key, rows, to in sums:
                        if target == when:
                            along(source, y).wait_recv()
                            emit(key, total(pos, rows) + yr[source].astype(F32), y + to)

    def grad_lane(lane, hop):
        for key in GRAD_HOPS:
            if key[1:] == (lane, hop):
                grad.arrived(*key)
                following = (*key[:2], hop + 1)
                if following in GRAD_HOPS:
                    start(grad.hop(*following))
                if key in THIRDS:
                    send_thirds(THIRDS.index(key))

    grad_lane(0, 1)
    third_arrived(len(THIRDS))
    for sign in (1, -1):
        start(grad.hop(sign, 2, 1))
    grad.swapped()
    for sign in (1, -1):
        start(grad.hop(sign, 1, 1))
    hidden_round(0, 1)
    grad_lane(2, 1)
    grad_lane(1, 1)
    weights(w_ref, part, 0, partner).wait_recv()
    start(weights(wo, part, 1, sibling))
    grad_lane(0, 2)
    hidden_round(0, 2)
    weights(wo, rest, 1, sibling).wait_recv()
    for hop in (0,):
        for pos in near_and_far(hop):
            product(pos)
    grad_lane(2, 2)
    grad_lane(1, 2)
    for hop in (1,):
        for pos in near_and_far(hop):
            product(pos)
    grad_lane(0, 3)
    hidden.swapped()
    for sign in (1, -1):
        start(hidden.hop(sign, 1, 1))
    hidden_round(0, 3)
    third_arrived(0)
    for hop in (2,):
        for pos in near_and_far(hop):
            product(pos)
    grad_lane(2, 3)
    grad_lane(1, 3)
    hidden_round(0, 4)
    third_arrived(1)
    third_arrived(2)
    for index in (0, 1):
        start(hidden.hand(index))
    for hop in (3,):
        for pos in near_and_far(hop):
            product(pos)
    hidden_round(1, 1)
    for which in (0, 1):
        grad_lane(which, 4)
    start(hidden.hand(2))
    third_arrived(3)
    for hop in (4,):
        for pos in near_and_far(hop):
            product(pos)
    heads = [key for far, key, _ in plans]
    for _, key, rows, to in sorted(singles, key=lambda m: m[1] not in heads):
        emit(key, total(y + _ , rows), y + to)
    for _, source, key, rows, to in sorted(sums, key=lambda m: m[1] not in heads):
        along(source, y).wait_recv()
        emit(key, total(y + _, rows) + yr[source].astype(F32), y + to)
    hidden_round(1, 2)
    for index in range(len(HANDED)):
        hidden.handed(index)
    acc[...] = jnp.zeros_like(acc)
    chunk = 4

    @pl.loop(0, 2 * RING // chunk)
    def _(step):
        tokens = pl.ds(step * chunk, chunk)
        left = ga[tokens].reshape(chunk * half, -1)
        right = ha[tokens].reshape(chunk * half, -1)
        acc[...] += lax.dot_general(
            left, right, (((0,), (0,)), ((), ())), preferred_element_type=F32
        )

    def to_sibling(src, dst, key):
        return pltpu.make_async_remote_copy(
            src_ref=src,
            dst_ref=dst,
            send_sem=d_send.at[key],
            recv_sem=d_recv.at[key],
            device_id=sibling,
            device_id_type=MESH,
        )

    weight_swap = to_sibling(acc, acc_in, 0)
    start(weight_swap)
    weight_swap.wait_recv()
    gw_ref[...] = (acc[...] + acc_in[...]).astype(BF16)

    for part in (0, 1):
        rows = pl.ds(part * quarter, quarter)
        value = total(y, rows)
        for far, key, which in plans:
            if which == part:
                for last in (key + 1, key + 3 if far == 4 else key + 2):
                    along(last, y).wait_recv()
                    value += yr[last].astype(F32)
        half_s[rows] = value.astype(BF16)
    half_swap = to_sibling(half_s, half_r, 1)
    start(half_swap)
    gh_ref[mine] = half_s[...]
    half_swap.wait_recv()
    gh_ref[pl.ds(pl.multiple_of((1 - depth) * half, half), half)] = half_r[...]
    for copy in sent:
        copy.wait_send()
    for key in range(messages):
        along(key, y).wait_send()
    @pl.when(lane != grad.lane)
    def _():
        for index in range(len(THIRDS) + 1):
            for copy in thirds(index):
                copy.wait_send()


def body(grad_out, hidden, weight):
    (tokens, features), units = grad_out.shape, hidden.shape[1]
    half, quarter, blocks = tokens // 2, tokens // 4, 2 * RING
    dma = pltpu.SemaphoreType.DMA
    vmem = pl.BlockSpec(memory_space=pltpu.VMEM)
    grads = len(GRAD_HOPS) + 3 + 2 * len(THIRDS)
    hiddens = len(HIDDEN_HOPS) + 1 + len(HANDED)
    return pl.pallas_call(
        kernel,
        out_shape=(
            jax.ShapeDtypeStruct(hidden.shape, BF16),
            jax.ShapeDtypeStruct(weight.shape, BF16),
        ),
        in_specs=[vmem] * 3,
        out_specs=(vmem, vmem),
        scratch_shapes=[
            pltpu.VMEM((blocks + RING, half, features), BF16),
            pltpu.VMEM((blocks, half, units), BF16),
            pltpu.VMEM(weight.shape, BF16),
            pltpu.VMEM((RING, half, units), F32),
            pltpu.VMEM((14, quarter, units), BF16),
            pltpu.VMEM((14, quarter, units), BF16),
            pltpu.VMEM((features, units), F32),
            pltpu.VMEM((features, units), F32),
            pltpu.VMEM((half, units), BF16),
            pltpu.VMEM((half, units), BF16),
            dma((grads,)), dma((grads,)), dma((hiddens,)), dma((hiddens,)),
            dma((2,)), dma((2,)), dma((14,)), dma((14,)), dma((2,)), dma((2,)),
        ],
        compiler_params=pltpu.CompilerParams(
            collective_id=0, has_side_effects=True, vmem_limit_bytes=56 << 20
        ),
    )(grad_out, hidden, weight)


def solution(mesh):
    return jax.shard_map(
        body,
        mesh=mesh,
        in_specs=(P("col", "row"), P("row", "col"), P("row", "col")),
        out_specs=(P("row", "col"), P("row", "col")),
        check_vma=False,
    )
```

```python
import jax
import jax.numpy as jnp
from jax import lax
from jax.experimental import pallas as pl
from jax.experimental.pallas import tpu as pltpu
from jax.sharding import PartitionSpec as P

MESH = pl.DeviceIdType.MESH
BF16, F32 = jnp.bfloat16, jnp.float32
RING = 8
GRAD_HOPS = [
    (sign, lane, hop)
    for hop in (1, 2, 3, 4)
    for lane in (0, 1, 2)
    for sign in (1, -1)
    if hop < 4 or (sign == 1) == (lane != 1)
]
HIDDEN_HOPS = [(1, 0, 1), (-1, 0, 1), (1, 0, 2), (-1, 0, 2), (1, 0, 3), (-1, 0, 3), (1, 0, 4)]
HIDDEN_HOPS += [(1, 1, 1), (-1, 1, 1), (-1, 1, 2)]
HANDED = [(1, 0, 2), (1, 0, 3), (-1, 0, 3), (1, 0, 4)]


def wrap(pos):
    return lax.rem(pos + RING, RING)


class Gather:
    def __init__(self, axis, hops, own, full, send, recv):
        at = lax.axis_index(axis)
        self.axis, self.hops, self.own, self.full = axis, hops, own, full
        self.send, self.recv = send, recv
        self.pos, self.lane = at // 2, lax.rem(at, 2)

    def device(self, pos, lane):
        return {self.axis: wrap(pos) * 2 + lane}

    def slot(self, pos, lane):
        if lane == 2:
            return 2 * RING + wrap(pos)
        return wrap(pos) * 2 + (1 - self.lane if lane else self.lane)

    def copy(self, src, slot, key, device):
        return pltpu.make_async_remote_copy(
            src_ref=src,
            dst_ref=self.full.at[slot],
            send_sem=self.send.at[key],
            recv_sem=self.recv.at[key],
            device_id=device,
            device_id_type=MESH,
        )

    def partner(self):
        return self.device(self.pos, 1 - self.lane)

    def swap(self):
        return self.copy(self.own, self.slot(self.pos, 0), len(self.hops), self.partner())

    def swapped(self):
        slot = self.slot(self.pos, 1)
        self.copy(self.full.at[slot], slot, len(self.hops), self.partner()).wait_recv()

    def hop(self, sign, lane, hop):
        slot = self.slot(self.pos - sign * (hop - 1), lane)
        src = self.own if hop == 1 and not lane else self.full.at[slot]
        key = self.hops.index((sign, lane, hop))
        return self.copy(src, slot, key, self.device(self.pos + sign, self.lane))

    def arrived(self, sign, lane, hop):
        slot = self.slot(self.pos - sign * hop, lane)
        key = self.hops.index((sign, lane, hop))
        device = self.device(self.pos - sign, self.lane)
        self.copy(self.full.at[slot], slot, key, device).wait_recv()

    def hand(self, index):
        sign, _, hop = HANDED[index]
        slot = self.slot(self.pos - sign * hop, 0)
        return self.copy(self.full.at[slot], slot, len(self.hops) + 1 + index, self.partner())

    def handed(self, index):
        sign, _, hop = HANDED[index]
        slot = self.slot(self.pos - sign * hop, 1)
        key = len(self.hops) + 1 + index
        self.copy(self.full.at[slot], slot, key, self.partner()).wait_recv()


def kernel(
    g_ref, h_ref, w_ref, gh_ref, gw_ref,
    ga, ha, wo, kept, ys, yr, acc, acc_in, half_s, half_r,
    g_send, g_recv, h_send, h_recv, w_send, w_recv, y_send, y_recv, d_send, d_recv,
):
    depth = lax.axis_index("depth")
    half = g_ref.shape[0] // 2
    quarter = half // 2
    mine = pl.ds(pl.multiple_of(depth * half, half), half)
    grad = Gather("col", GRAD_HOPS, g_ref.at[mine], ga, g_send, g_recv)
    hidden = Gather("row", HIDDEN_HOPS, h_ref.at[mine], ha, h_send, h_recv)
    y, lane = hidden.pos, hidden.lane

    def row_device(pos):
        return {"row": wrap(pos) * 2 + lane}

    partner = hidden.partner()
    sibling = {"depth": 1 - depth}
    across = partner | grad.partner()

    barrier = pltpu.get_barrier_semaphore()
    peers = [partner, sibling, across, grad.partner()]
    peers += [grad.device(grad.pos + k, grad.lane) for k in (-1, 1)]
    peers += [row_device(y + k) for k in (-3, -2, -1, 1, 2, 3)]
    for peer in peers:
        pl.semaphore_signal(barrier, inc=1, device_id=peer, device_id_type=MESH)
    pl.semaphore_wait(barrier, len(peers))

    sent = []

    def start(copy):
        copy.start()
        sent.append(copy)

    lane_2 = len(GRAD_HOPS) + 1
    third = [grad.copy(grad.own, grad.slot(grad.pos, 2), lane_2 + i, to) for i, to in enumerate((partner, across))]

    def third_arrived():
        slot = grad.slot(grad.pos, 2)
        for i, (source, here) in enumerate(((partner, lane == grad.lane), (across, lane != grad.lane))):
            @pl.when(here)
            def _():
                grad.copy(ga.at[slot], slot, lane_2 + i, source).wait_recv()

    features = w_ref.shape[0] // 2
    part = pl.ds(pl.multiple_of(depth * features, features), features)
    rest = pl.ds(pl.multiple_of((1 - depth) * features, features), features)

    def weights(src, rows, key, device):
        return pltpu.make_async_remote_copy(
            src_ref=src.at[rows],
            dst_ref=wo.at[rows],
            send_sem=w_send.at[key],
            recv_sem=w_recv.at[key],
            device_id=device,
            device_id_type=MESH,
        )

    for sign in (1, -1):
        start(grad.hop(sign, 0, 1))
    @pl.when(lane != grad.lane)
    def _():
        for copy in third:
            copy.start()
    start(grad.swap())
    for sign in (1, -1):
        start(hidden.hop(sign, 0, 1))
    for gather in (grad, hidden):
        gather.full[gather.slot(gather.pos, 0)] = gather.own[...]

    def hidden_round(lane, hop):
        for key in HIDDEN_HOPS:
            if key[1:] == (lane, hop):
                hidden.arrived(*key)
                following = (*key[:2], hop + 1)
                if following in HIDDEN_HOPS:
                    start(hidden.hop(*following))
                if key in HANDED:
                    start(hidden.hand(HANDED.index(key)))

    def product(pos):
        pos = wrap(pos)
        value = jnp.dot(ga[pos * 2 + lane], w_ref[...], preferred_element_type=F32)
        kept[pos] = value + jnp.dot(ga[2 * RING + pos], wo[...], preferred_element_type=F32)

    def total(pos, rows):
        return kept[wrap(pos), rows]

    plans, singles, sums, at = [], [], [], 0
    for sign in (1, -1):
        for piece in (0, 1):
            far = 4 if (piece == 0) == (sign == 1) else 3
            rows = pl.ds(piece * quarter, quarter)
            plans.append((far, at, piece))
            singles.append((sign * far % RING, at, rows, sign))
            sums.append((sign * (far - 1) % RING, at, at + 1, rows, sign * (far - 1)))
            if far == 4:
                singles.append((sign * 2 % RING, at + 2, rows, sign))
                sums.append((sign % RING, at + 2, at + 3, rows, sign))
            else:
                singles.append((sign % RING, at + 2, rows, sign))
            at += far
    messages = at

    def along(key, pos):
        return pltpu.make_async_remote_copy(
            src_ref=ys.at[key],
            dst_ref=yr.at[key],
            send_sem=y_send.at[key],
            recv_sem=y_recv.at[key],
            device_id=row_device(pos),
            device_id_type=MESH,
        )

    def emit(key, value, pos):
        ys[key] = value.astype(BF16)
        along(key, pos).start()

    def near_and_far(hop):
        return [grad.pos - hop] + ([grad.pos + hop] if 0 < hop < 4 else [])

    def send_singles(hop):
        for pos in near_and_far(hop):
            product(pos)
            place = lax.rem(wrap(pos) - y + RING, RING)
            for when in range(1, RING):
                @pl.when(place == when)
                def _():
                    for target, key, rows, to in singles:
                        if target == when:
                            emit(key, total(pos, rows), y + to)

    def send_sums(hop):
        for pos in near_and_far(hop):
            place = lax.rem(wrap(pos) - y + RING, RING)
            for when in range(1, RING):
                @pl.when(place == when)
                def _():
                    for target, source, key, rows, to in sums:
                        if target == when:
                            along(source, y).wait_recv()
                            emit(key, total(pos, rows) + yr[source].astype(F32), y + to)

    def grad_lane(lane, hop):
        for key in GRAD_HOPS:
            if key[1:] == (lane, hop):
                grad.arrived(*key)
                following = (*key[:2], hop + 1)
                if following in GRAD_HOPS:
                    start(grad.hop(*following))

    grad_lane(0, 1)
    third_arrived()
    for sign in (1, -1):
        start(grad.hop(sign, 2, 1))
    grad.swapped()
    start(weights(w_ref, part, 0, partner))
    for sign in (1, -1):
        start(grad.hop(sign, 1, 1))
    hidden_round(0, 1)
    grad_lane(2, 1)
    grad_lane(1, 1)
    weights(w_ref, part, 0, partner).wait_recv()
    start(weights(wo, part, 1, sibling))
    start(hidden.swap())
    grad_lane(0, 2)
    hidden_round(0, 2)
    weights(wo, rest, 1, sibling).wait_recv()
    for hop in (0,):
        for pos in near_and_far(hop):
            product(pos)
    grad_lane(2, 2)
    grad_lane(1, 2)
    for hop in (1,):
        for pos in near_and_far(hop):
            product(pos)
    grad_lane(0, 3)
    hidden.swapped()
    for sign in (1, -1):
        start(hidden.hop(sign, 1, 1))
    hidden_round(0, 3)
    for hop in (2,):
        for pos in near_and_far(hop):
            product(pos)
    grad_lane(2, 3)
    grad_lane(1, 3)
    hidden_round(0, 4)
    for hop in (3,):
        for pos in near_and_far(hop):
            product(pos)
    hidden_round(1, 1)
    for which in (0, 2, 1):
        grad_lane(which, 4)
    for hop in (4,):
        for pos in near_and_far(hop):
            product(pos)
    chains, at = [], 0
    for far, _, piece in plans:
        sign = 1 if (piece == 0) == (far == 4) else -1
        chains.append((sign, pl.ds(piece * quarter, quarter), far, at))
        at += far
    for step in range(4):
        for sign, rows, far, key in chains:
            if step < far:
                value = total(y + sign * (far - step), rows)
                if step:
                    along(key + step - 1, y).wait_recv()
                    value += yr[key + step - 1].astype(F32)
                emit(key + step, value, y + sign)

    hidden_round(1, 2)
    for index in range(len(HANDED)):
        hidden.handed(index)
    acc[...] = jnp.zeros_like(acc)
    chunk = 4

    @pl.loop(0, 2 * RING // chunk)
    def _(step):
        tokens = pl.ds(step * chunk, chunk)
        left = ga[tokens].reshape(chunk * half, -1)
        right = ha[tokens].reshape(chunk * half, -1)
        acc[...] += lax.dot_general(
            left, right, (((0,), (0,)), ((), ())), preferred_element_type=F32
        )

    def to_sibling(src, dst, key):
        return pltpu.make_async_remote_copy(
            src_ref=src,
            dst_ref=dst,
            send_sem=d_send.at[key],
            recv_sem=d_recv.at[key],
            device_id=sibling,
            device_id_type=MESH,
        )

    weight_swap = to_sibling(acc, acc_in, 0)
    start(weight_swap)
    weight_swap.wait_recv()
    gw_ref[...] = (acc[...] + acc_in[...]).astype(BF16)

    for part in (0, 1):
        rows = pl.ds(part * quarter, quarter)
        value = total(y, rows)
        for far, key, which in plans:
            if which == part:
                for last in (key + far - 1,):
                    along(last, y).wait_recv()
                    value += yr[last].astype(F32)
        half_s[rows] = value.astype(BF16)
    half_swap = to_sibling(half_s, half_r, 1)
    start(half_swap)
    gh_ref[mine] = half_s[...]
    half_swap.wait_recv()
    gh_ref[pl.ds(pl.multiple_of((1 - depth) * half, half), half)] = half_r[...]
    for copy in sent:
        copy.wait_send()
    for key in range(messages):
        along(key, y).wait_send()
    @pl.when(lane != grad.lane)
    def _():
        for copy in third:
            copy.wait_send()


def body(grad_out, hidden, weight):
    (tokens, features), units = grad_out.shape, hidden.shape[1]
    half, quarter, blocks = tokens // 2, tokens // 4, 2 * RING
    dma = pltpu.SemaphoreType.DMA
    vmem = pl.BlockSpec(memory_space=pltpu.VMEM)
    grads = len(GRAD_HOPS) + 3
    hiddens = len(HIDDEN_HOPS) + 1 + len(HANDED)
    return pl.pallas_call(
        kernel,
        out_shape=(
            jax.ShapeDtypeStruct(hidden.shape, BF16),
            jax.ShapeDtypeStruct(weight.shape, BF16),
        ),
        in_specs=[vmem] * 3,
        out_specs=(vmem, vmem),
        scratch_shapes=[
            pltpu.VMEM((blocks + RING, half, features), BF16),
            pltpu.VMEM((blocks, half, units), BF16),
            pltpu.VMEM(weight.shape, BF16),
            pltpu.VMEM((RING, half, units), F32),
            pltpu.VMEM((14, quarter, units), BF16),
            pltpu.VMEM((14, quarter, units), BF16),
            pltpu.VMEM((features, units), F32),
            pltpu.VMEM((features, units), F32),
            pltpu.VMEM((half, units), BF16),
            pltpu.VMEM((half, units), BF16),
            dma((grads,)), dma((grads,)), dma((hiddens,)), dma((hiddens,)),
            dma((2,)), dma((2,)), dma((14,)), dma((14,)), dma((2,)), dma((2,)),
        ],
        compiler_params=pltpu.CompilerParams(
            collective_id=0, has_side_effects=True, vmem_limit_bytes=56 << 20
        ),
    )(grad_out, hidden, weight)


def solution(mesh):
    return jax.shard_map(
        body,
        mesh=mesh,
        in_specs=(P("col", "row"), P("row", "col"), P("row", "col")),
        out_specs=(P("row", "col"), P("row", "col")),
        check_vma=False,
    )
```
